32 devices in a mesh: table: 8 (over z, y), col: 4 (over x, core).
Axes of the slice: x: 2, y: 2, z: 4, core: 2. Of those that a mesh axis runs over, the one named last changes fastest.
Arguments:
- embedding: bfloat16 [32768, 256], P('table', 'col'), may hold values from -4 to 4
- accumulator: float32 [32768, 256], P('table', 'col'), may hold values from 0.01 to 1
- pair_rows: int32 [256, 128, 4], P(('table', 'col')), may hold values from 0 to 1023
- pair_len: int32 [256, 128], P(('table', 'col')), may hold values from 0 to 4
- pair_dest: int32 [32, 8], P(('table', 'col')), may hold values from 0 to 7, each once within a row
- pair_tile: int32 [32, 8], P(('table', 'col')), may hold values from 0 to 15
- pooled_grad: bfloat16 [65536, 256], P(('table', 'col')), may hold values from -6 to 6
Outputs:
- pooled: bfloat16 [65536, 256], P(('table', 'col'))
- new_embedding: bfloat16 [32768, 256], P(('table', 'col'))
- new_accumulator: float32 [32768, 256], P(('table', 'col'))
The draws below stay inside these ranges and needn't reach their ends.
Inputs may be any that keep to these rules, and one draw needn't show every extreme that they name: `pair_dest`: each row names every table index exactly once.
All inputs are finite; a program needn't handle non-finite values.
Results may differ from the reference program's by a relative error of at most 0.0049.
Values may be sent and summed in bfloat16 or wider, within the bound.
No kernel may reach another device: no remote copies, remote signals or barrier semaphores. Data moves between devices by JAX's collectives and lax.ppermute only.
A program may use at most 128 MiB of HBM per device.

```python
import math
import jax
import jax.numpy as jnp
from jax import lax

DIM = 256
BLOCK = 128
LOOK = 4
R_DEV = 1024
TILE_DEV = 16
PAIRS = 8
ROWS = 32768
BAGS = 65536
N_TABLE = 8
N_COL = 4
DEVICES = 32


def touch_ends(drawn, stream_key, smallest, high):
    longest = drawn.shape.index(max(drawn.shape))
    spots = []
    for shift in (0, 1):
        where = [jax.random.randint(jax.random.fold_in(stream_key, axis), (), 0, length) for axis, length in enumerate(drawn.shape)]
        where[longest] = (where[longest] + shift) % drawn.shape[longest]
        spots.append(tuple(where))
    return drawn.at[spots[0]].set(smallest).at[spots[1]].set(high)


def block_scale(stream_key, extent, shards, smallest, top_value):
    loudness, own = 1.0, jax.random.fold_in(stream_key, 6)
    for dim, shards_of in shards:
        draws = jnp.exp(jax.random.uniform(jax.random.fold_in(own, dim), (shards_of,), jnp.float32, smallest / len(shards), top_value / len(shards)))
        loudness = loudness * jnp.repeat(draws, extent[dim] // shards_of).reshape([-1 if axis == dim else 1 for axis in range(len(extent))])
    return loudness


def centred(own_key, extent, deviation, reach, pieces=(), held_as=jnp.bfloat16):
    entries = deviation * jax.random.normal(own_key, extent, jnp.float32)
    if pieces:
        entries = entries * block_scale(own_key, extent, pieces, -0.22, 0.18)
    return jnp.clip(entries, -reach, reach).astype(held_as)


def setup_inputs(seed: int = 0) -> dict:
    key_of = jax.random.split(jax.random.key(seed), 8)
    return {
        "embedding": centred(key_of[0], (ROWS, DIM), 0.5, 4.0, ((0, 8), (1, 4))),
        "accumulator": jnp.clip(jnp.exp(math.log(1.0) - 4.6051702 * jax.random.uniform(key_of[1], (ROWS, DIM), jnp.float32) ** block_scale(key_of[1], (ROWS, DIM), ((0, 8), (1, 4)), -0.2, 0.2)), 0.01, 1.0),
        "pair_rows": touch_ends(jax.random.randint(key_of[2], (DEVICES * PAIRS, BLOCK, LOOK), 0, R_DEV), jax.random.fold_in(key_of[2], 1), 0, R_DEV - 1).astype(jnp.int32),
        "pair_len": touch_ends(jax.random.randint(key_of[3], (DEVICES * PAIRS, BLOCK), 0, LOOK + 1), jax.random.fold_in(key_of[3], 1), 0, LOOK).astype(jnp.int32),
        "pair_dest": jax.vmap(lambda own: jax.random.permutation(own, N_TABLE))(jax.random.split(key_of[4], DEVICES)).reshape((DEVICES, PAIRS)).astype(jnp.int32),
        "pair_tile": touch_ends(jax.random.randint(key_of[5], (DEVICES, PAIRS), 0, TILE_DEV), jax.random.fold_in(key_of[5], 1), 0, TILE_DEV - 1).astype(jnp.int32),
        "pooled_grad": centred(key_of[6], (BAGS, DIM), 1.0, 6.0, ((0, 32),)),
    }


def reference(embedding, accumulator, pair_rows, pair_len, pair_dest, pair_tile, pooled_grad):
    device_count = N_TABLE * N_COL
    rows_all = pair_rows.reshape(device_count, PAIRS, BLOCK, LOOK)
    lens_all = pair_len.reshape(device_count, PAIRS, BLOCK)
    emb_all = embedding.reshape(device_count, R_DEV, DIM)
    acc_all = accumulator.reshape(device_count, R_DEV, DIM)
    grad_tiles = pooled_grad.reshape(device_count * TILE_DEV, BLOCK, DIM)
    owner_ids = jnp.arange(device_count, dtype=jnp.int32)

    def per_owner(total, item):
        owner, emb_rows, acc_rows, rows, lens, dests, tiles = item
        valid = (jnp.arange(LOOK, dtype=jnp.int32)[None, None, :] < lens[:, :, None]).astype(jnp.float32)
        picked = emb_rows[rows].astype(jnp.float32) * valid[..., None]
        partial_value = lax.optimization_barrier(jnp.sum(picked, axis=2)).astype(jnp.bfloat16)
        global_tile = ((dests * N_COL + owner % N_COL) * TILE_DEV + tiles).astype(jnp.int32)
        total = total.at[global_tile].add(partial_value.astype(jnp.float32))
        cot = grad_tiles[global_tile].astype(jnp.float32)
        contrib = cot[:, :, None, :] * valid[..., None]
        grad = jnp.zeros((R_DEV, DIM), jnp.float32).at[rows.reshape(-1)].add(contrib.reshape(-1, DIM))
        new_acc = acc_rows + grad * grad
        new_emb = (emb_rows.astype(jnp.float32) - 0.3 * grad / (jnp.sqrt(new_acc) + 1e-08)).astype(jnp.bfloat16)
        return (total, (new_emb, new_acc))
    start = jnp.zeros((device_count * TILE_DEV, BLOCK, DIM), jnp.float32)
    total, outs = lax.scan(per_owner, start, (owner_ids, emb_all, acc_all, rows_all, lens_all, pair_dest, pair_tile))
    pooled = total.reshape(BAGS, DIM).astype(jnp.bfloat16)
    return (pooled, outs[0].reshape(ROWS, DIM), outs[1].reshape(ROWS, DIM))
```

```python
import functools

import jax
import jax.numpy as jnp
from jax import lax
from jax.experimental import pallas as pl
from jax.experimental.pallas import tpu as pltpu
from jax.sharding import PartitionSpec as P

LEARN_RATE = 0.3
EPSILON = 1e-08
MARK_ROWS = 8

VMEM = pl.BlockSpec(memory_space=pltpu.VMEM)
SMEM = pl.BlockSpec(memory_space=pltpu.SMEM)


def even(n):
    return n & (n - 1) == 0


def target(i, k, n):
    return i ^ k if even(n) else (i + k) % n


def origin(i, k, n):
    return i ^ k if even(n) else (i + n - k) % n


def step_of(j, i, n):
    return j ^ i if even(n) else lax.rem(j + n - i, n)


def steps(n):
    return sorted(range(1, n), key=lambda k: (-k.bit_length(), k))


def pairs_of(k, n):
    return [(i, target(i, k, n)) for i in range(n)]


def back_of(k, n):
    return [(j, i) for i, j in pairs_of(k, n)]


def call(body, out_shape, in_specs, out_specs, args, scratch=(), limit=None, flops=0, name=None):
    size = sum(a.size * a.dtype.itemsize for a in args) + sum(
        o.size * o.dtype.itemsize for o in jax.tree.leaves(out_shape)
    )
    return pl.pallas_call(
        body,
        out_shape=out_shape,
        in_specs=in_specs,
        out_specs=out_specs,
        scratch_shapes=scratch,
        compiler_params=pltpu.CompilerParams(vmem_limit_bytes=limit),
        cost_estimate=pl.CostEstimate(flops=flops, bytes_accessed=size, transcendentals=0),
        name=name,
    )(*args)


def split_body(count, rows, where_ref, wide_ref, *outs):
    for k in range(count):
        start = pl.multiple_of(where_ref[k] * rows, rows)
        outs[k][...] = wide_ref[:, pl.ds(start, rows)].astype(outs[k].dtype)


def count_body(rows_ref, lens_ref, counts_ref):
    pairs, looks, bags = rows_ref.shape
    width = counts_ref.shape[0]

    def one(p, carry):
        line = lax.broadcasted_iota(jnp.int32, (width, bags), 0)
        lens = lens_ref[pl.ds(p, 1), :]
        total = jnp.zeros((width, bags), jnp.float32)
        for look in range(looks):
            row = rows_ref[p, pl.ds(look, 1), :]
            row = jnp.where(lens > look, row, -1)
            total = total + (line == row).astype(jnp.float32)
        counts_ref[:, pl.ds(pl.multiple_of(p * bags, bags), bags)] = total.astype(jnp.bfloat16)
        return carry

    lax.fori_loop(0, pairs, one, 0)


def pool_body(tables, cols, span, spot_ref, dest_ref, tile_ref, counts_ref, *refs):
    slabs, outs = refs[:cols], refs[cols : cols + tables]
    wide_ref, parts_ref, pair_ref = refs[cols + tables :]
    thin = slabs[0].shape[0]
    bags = parts_ref.shape[1]
    width = wide_ref.shape[0]
    pairs = dest_ref.shape[1]
    me = spot_ref[0]
    for p in range(pairs):
        pair_ref[step_of(dest_ref[0, p], me, tables)] = p
    for k in range(cols):
        first = pl.multiple_of(spot_ref[1 + k] * thin, thin)
        wide_ref[pl.ds(first, thin), :] = slabs[k][...]
    wide = wide_ref[...]

    def group(g, carry):
        first = pl.multiple_of(g * span * bags, span * bags)
        part = jnp.dot(
            wide, counts_ref[:, pl.ds(first, span * bags)], preferred_element_type=jnp.float32
        )
        for s in range(span):
            parts_ref[g * span + s] = part[:, s * bags : (s + 1) * bags].T.astype(jnp.bfloat16)
        return carry

    lax.fori_loop(0, pairs // span, group, 0)
    outs[0][...] = parts_ref[pair_ref[0]]
    lane = lax.broadcasted_iota(jnp.int32, (MARK_ROWS, width), 1)
    half = width // 2
    for k in range(1, tables):
        p = pair_ref[k]
        tile = tile_ref[0, p]
        outs[k][:bags, :] = parts_ref[p]
        mark = jnp.where(lane < half, tile % 128, tile // 128)
        outs[k][bags:, :] = mark.astype(jnp.float32).astype(jnp.bfloat16)


def read_mark(mark_ref):
    mark = mark_ref[...].astype(jnp.float32)
    half = mark.shape[1] // 2
    low = jnp.max(mark[:, :half]).astype(jnp.int32)
    high = jnp.max(mark[:, half:]).astype(jnp.int32)
    return high * 128 + low


def pick_body(count, bags, *refs):
    marks, grad_ref, outs = refs[:count], refs[count], refs[count + 1 :]
    for k in range(count):
        tile = read_mark(marks[k].at[pl.ds(bags, MARK_ROWS)])
        outs[k][...] = grad_ref[pl.ds(pl.multiple_of(tile * bags, bags), bags), :]


def sum_body(tables, own_tile_ref, own_ref, *refs):
    blocks, out_ref, total_ref = refs[: tables - 1], refs[tables - 1], refs[tables]
    bags = own_ref.shape[0]
    total_ref[...] = jnp.zeros_like(total_ref)

    def add(tile, block):
        where = pl.ds(pl.multiple_of(tile * bags, bags), bags)
        total_ref[where, :] += block.astype(jnp.float32)

    add(own_tile_ref[0], own_ref[...])
    for block_ref in blocks:
        tile = read_mark(block_ref.at[pl.ds(bags, MARK_ROWS)])
        add(tile, block_ref[:bags, :])
    out_ref[...] = total_ref[...].astype(jnp.bfloat16)


def turn_body(cols, spot_ref, *refs):
    slabs, states = refs[:cols], refs[cols : 2 * cols]
    rows_ref, state_ref, wide_ref = refs[2 * cols :]
    thin = slabs[0].shape[0]
    for source, out_ref in ((slabs, rows_ref), (states, state_ref)):
        for k in range(cols):
            first = pl.multiple_of(spot_ref[1 + k] * thin, thin)
            wide_ref[pl.ds(first, thin), :] = source[k][...].astype(jnp.float32)
        out_ref[...] = wide_ref[...].T.astype(out_ref.dtype)


def update_body(tables, chunk, spot_ref, own_tile_ref, dest_ref, grad_ref, counts_ref, rows_ref, state_ref, *refs):
    blocks = refs[: tables - 1]
    new_rows_ref, new_state_ref, cots_ref, pair_ref = refs[tables - 1 :]
    bags = blocks[0].shape[0]
    me = spot_ref[0]
    for p in range(dest_ref.shape[1]):
        pair_ref[step_of(dest_ref[0, p], me, tables)] = p

    def put(k, block):
        first = pl.multiple_of(pair_ref[k] * bags, bags)
        cots_ref[pl.ds(first, bags), :] = block

    put(0, grad_ref[pl.ds(pl.multiple_of(own_tile_ref[0] * bags, bags), bags), :])
    for k in range(1, tables):
        put(k, blocks[k - 1][...])

    def one(r, carry):
        where = pl.ds(pl.multiple_of(r * chunk, chunk), chunk)
        grad = jnp.dot(counts_ref[where, :], cots_ref[...], preferred_element_type=jnp.float32)
        state = state_ref[where, :].astype(jnp.float32) + grad * grad
        rows = rows_ref[where, :].astype(jnp.float32)
        new_state_ref[where, :] = state
        new_rows_ref[where, :] = (
            rows - LEARN_RATE * grad / (jnp.sqrt(state) + EPSILON)
        ).astype(jnp.bfloat16)
        return carry

    lax.fori_loop(0, counts_ref.shape[0] // chunk, one, 0)


def per_device(embedding, accumulator, pair_rows, pair_len, pair_dest, pair_tile, pooled_grad):
    tables, cols = lax.axis_size("table"), lax.axis_size("col")
    me_table, me_col = lax.axis_index("table"), lax.axis_index("col")
    pairs, bags, looks = pair_rows.shape
    thin = embedding.shape[1]
    width = thin * cols
    rows = embedding.shape[0] // cols
    span = min(8, pairs)
    chunk = min(256, rows)
    shape = jax.ShapeDtypeStruct
    bf16 = jnp.bfloat16
    mega = 1 << 20
    spare = pairs * bags * width * 2
    big = 4 * mega + rows * pairs * bags * 2 + 4 * spare + 12 * rows * width

    send_at = jnp.stack([target(me_col, k, cols) for k in range(cols)]).astype(jnp.int32)
    spot = jnp.stack([me_table] + [origin(me_col, k, cols) for k in range(cols)]).astype(jnp.int32)

    def split(wide):
        return call(
            functools.partial(split_body, cols, rows),
            [shape((thin, rows), bf16)] * cols,
            [SMEM, VMEM],
            [VMEM] * cols,
            (send_at, wide),
            limit=16 * mega,
            name="split",
        )

    def over_col(parts):
        return [parts[0]] + [lax.ppermute(parts[k], "col", pairs_of(k, cols)) for k in range(1, cols)]

    slabs = over_col(split(embedding.T))
    states = over_col(split(accumulator.T))

    counts = call(
        count_body,
        shape((rows, pairs * bags), bf16),
        [VMEM, VMEM],
        VMEM,
        (jnp.transpose(pair_rows, (0, 2, 1)), pair_len),
        limit=8 * mega + rows * pairs * bags * 2,
        name="count",
    )

    sent = call(
        functools.partial(pool_body, tables, cols, span),
        [shape((bags, width), bf16)] + [shape((bags + MARK_ROWS, width), bf16)] * (tables - 1),
        [SMEM, SMEM, SMEM, VMEM] + [VMEM] * cols,
        [VMEM] * tables,
        (spot, pair_dest, pair_tile, counts, *slabs),
        scratch=[
            pltpu.VMEM((width, rows), bf16),
            pltpu.VMEM((pairs, bags, width), bf16),
            pltpu.SMEM((pairs,), jnp.int32),
        ],
        limit=big,
        flops=2 * rows * width * pairs * bags,
        name="pool",
    )
    own_block = sent[0]
    order = steps(tables)
    arrived = {k: lax.ppermute(sent[k], "table", pairs_of(k, tables)) for k in order}

    grad_spec = VMEM
    returned = {}
    far = [order[i : i + 2] for i in range(0, len(order) // 2 + 1, 2)]
    taken = sum(len(g) for g in far)
    groups = far + ([order[taken:]] if taken < len(order) else [])
    for ks in groups:
        picked = call(
            functools.partial(pick_body, len(ks), bags),
            [shape((bags, width), bf16)] * len(ks),
            [VMEM] * len(ks) + [grad_spec],
            [VMEM] * len(ks),
            (*[arrived[k] for k in ks], pooled_grad),
            limit=8 * mega + 2 * spare,
            name="pick",
        )
        for k, block in zip(ks, picked, strict=True):
            returned[k] = lax.ppermute(block, "table", back_of(k, tables))

    own_tile = jnp.sum(jnp.where(pair_dest[0] == me_table, pair_tile[0], 0)).reshape(1)
    pooled = call(
        functools.partial(sum_body, tables),
        shape(pooled_grad.shape, bf16),
        [SMEM, VMEM] + [VMEM] * (tables - 1),
        VMEM,
        (own_tile, own_block, *[arrived[k] for k in range(1, tables)]),
        scratch=[pltpu.VMEM(pooled_grad.shape, jnp.float32)],
        limit=8 * mega + 2 * spare,
        name="sum",
    )

    turned = call(
        functools.partial(turn_body, cols),
        [shape((rows, width), bf16), shape((rows, width), bf16)],
        [SMEM] + [VMEM] * (2 * cols),
        [VMEM, VMEM],
        (spot, *slabs, *states),
        scratch=[pltpu.VMEM((width, rows), jnp.float32)],
        limit=16 * mega,
        name="turn",
    )
    new_rows, new_state = call(
        functools.partial(update_body, tables, chunk),
        [shape((rows, width), bf16), shape((rows, width), jnp.float32)],
        [SMEM, SMEM, SMEM, VMEM, VMEM, VMEM, VMEM] + [VMEM] * (tables - 1),
        [VMEM, VMEM],
        (spot, own_tile, pair_dest, pooled_grad, counts, *turned, *[returned[k] for k in range(1, tables)]),
        scratch=[pltpu.VMEM((pairs * bags, width), bf16), pltpu.SMEM((pairs,), jnp.int32)],
        limit=big,
        flops=2 * rows * width * pairs * bags,
        name="update",
    )
    return (pooled, new_rows, new_state)


def solution(mesh):
    return jax.shard_map(
        per_device,
        mesh=mesh,
        in_specs=(
            P("table", "col"),
            P("table", "col"),
            P(("table", "col"), None, None),
            P(("table", "col"), None),
            P(("table", "col"), None),
            P(("table", "col"), None),
            P(("table", "col"), None),
        ),
        out_specs=(P(("table", "col"), None), P(("table", "col"), None), P(("table", "col"), None)),
        check_vma=False,
    )
```

```python
import functools

import jax
import jax.numpy as jnp
from jax import lax
from jax.experimental import pallas as pl
from jax.experimental.pallas import tpu as pltpu
from jax.sharding import PartitionSpec as P


LEARN_RATE = 0.3
EPSILON = 1e-08
MARK_ROWS = 8

ANY = pl.BlockSpec(memory_space=pl.ANY)
HBM = pl.BlockSpec(memory_space=pltpu.HBM)
VMEM = pl.BlockSpec(memory_space=pltpu.VMEM)
SMEM = pl.BlockSpec(memory_space=pltpu.SMEM)


def even(n):
    return n & (n - 1) == 0


def target(i, k, n):
    return i ^ k if even(n) else (i + k) % n


def origin(i, k, n):
    return i ^ k if even(n) else (i + n - k) % n


def step_of(j, i, n):
    return j ^ i if even(n) else lax.rem(j + n - i, n)


def steps(n):
    return sorted(range(1, n), key=lambda k: (-k.bit_length(), k))


def pairs_of(k, n):
    return [(i, target(i, k, n)) for i in range(n)]


def back_of(k, n):
    return [(j, i) for i, j in pairs_of(k, n)]


def call(body, out_shape, in_specs, out_specs, args, scratch=(), limit=None, flops=0):
    size = sum(a.size * a.dtype.itemsize for a in args)
    return pl.pallas_call(
        body,
        out_shape=out_shape,
        in_specs=in_specs,
        out_specs=out_specs,
        scratch_shapes=scratch,
        compiler_params=pltpu.CompilerParams(vmem_limit_bytes=limit),
        cost_estimate=pl.CostEstimate(flops=flops, bytes_accessed=size, transcendentals=0),
    )(*args)


def far(x):
    return pltpu.with_memory_space_constraint(x, pltpu.HBM)


def sequence(n):
    top = [k for k in range(1, n) if 2 * k >= n]
    low = [k for k in range(1, n) if 2 * k < n]
    mixed = []
    while top or low:
        mixed += top[:1] + low[:1]
        top, low = top[1:], low[1:]
    return [("part", k) for k in mixed] + [("cot", k) for k in mixed]


def split_body(count, rows, wide_ref, *refs):
    outs, sems = refs[:count], refs[count]
    me = lax.axis_index("col")
    copies = []
    for k in range(count):
        start = pl.multiple_of(target(me, k, count) * rows, rows)
        copies.append(pltpu.make_async_copy(wide_ref.at[:, pl.ds(start, rows)], outs[k], sems.at[k]))
        copies[k].start()
    for copy in copies:
        copy.wait()


def count_body(cols, wide_ref, rows_hbm, lens_hbm, counts_ref, *refs):
    outs = refs[:cols]
    rows_ref, lens_ref, slab_ref, sems = refs[cols:]
    pairs, looks, bags = rows_ref.shape
    width = counts_ref.shape[0]
    me = lax.axis_index("col")
    rows_copy = pltpu.make_async_copy(rows_hbm, rows_ref, sems.at[cols])
    lens_copy = pltpu.make_async_copy(lens_hbm, lens_ref, sems.at[cols + 1])
    rows_copy.start()
    lens_copy.start()
    copies = []
    for k in range(cols):
        start = pl.multiple_of(target(me, k, cols) * width, width)
        copies.append(
            pltpu.make_async_copy(wide_ref.at[:, pl.ds(start, width)], slab_ref.at[k], sems.at[k])
        )
        copies[k].start()
    rows_copy.wait()
    lens_copy.wait()

    def one(p, carry):
        line = lax.broadcasted_iota(jnp.int32, (width, bags), 0)
        lens = lens_ref[pl.ds(p, 1), :]
        total = jnp.zeros((width, bags), jnp.float32)
        for look in range(looks):
            row = rows_ref[p, pl.ds(look, 1), :]
            row = jnp.where(lens > look, row, -1)
            total = total + (line == row).astype(jnp.float32)
        counts_ref[:, pl.ds(pl.multiple_of(p * bags, bags), bags)] = total.astype(jnp.bfloat16)
        return carry

    lax.fori_loop(0, pairs, one, 0)
    for k in range(cols):
        copies[k].wait()
        outs[k][...] = slab_ref[k].astype(jnp.bfloat16)


def pool_body(tables, cols, span, plan_ref, counts_ref, *refs):
    slabs, outs = refs[:cols], refs[cols : cols + tables]
    wide_ref, parts_ref, pair_ref = refs[cols + tables :]
    thin = slabs[0].shape[0]
    bags = parts_ref.shape[1]
    width = wide_ref.shape[0]
    pairs = plan_ref.shape[1]
    me = lax.axis_index("table")
    for p in range(pairs):
        pair_ref[step_of(plan_ref[0, p], me, tables)] = p
    here = lax.axis_index("col")
    for k in range(cols):
        first = pl.multiple_of(origin(here, k, cols) * thin, thin)
        wide_ref[pl.ds(first, thin), :] = slabs[k][...]
    wide = wide_ref[...]

    def group(g, carry):
        first = pl.multiple_of(g * span * bags, span * bags)
        part = jnp.dot(
            wide, counts_ref[:, pl.ds(first, span * bags)], preferred_element_type=jnp.float32
        )
        for s in range(span):
            parts_ref[g * span + s] = part[:, s * bags : (s + 1) * bags].T.astype(jnp.bfloat16)
        return carry

    lax.fori_loop(0, pairs // span, group, 0)
    outs[0][...] = parts_ref[pair_ref[0]]
    lane = lax.broadcasted_iota(jnp.int32, (MARK_ROWS, width), 1)
    half = width // 2
    for k in range(1, tables):
        p = pair_ref[k]
        tile = plan_ref[1, p]
        outs[k][:bags, :] = parts_ref[p]
        mark = jnp.where(lane < half, tile % 128, tile // 128)
        outs[k][bags:, :] = mark.astype(jnp.float32).astype(jnp.bfloat16)


def read_mark(mark_ref):
    mark = mark_ref[...].astype(jnp.float32)
    half = mark.shape[1] // 2
    low = jnp.max(mark[:, :half]).astype(jnp.int32)
    high = jnp.max(mark[:, half:]).astype(jnp.int32)
    return high * 128 + low


def pick_body(count, bags, *refs):
    marks, grad_ref, outs = refs[:count], refs[count], refs[count + 1 :]
    for k in range(count):
        tile = read_mark(marks[k].at[pl.ds(bags, MARK_ROWS)])
        outs[k][...] = grad_ref[pl.ds(pl.multiple_of(tile * bags, bags), bags), :]


def own_tile(plan_ref):
    tile, me = 0, lax.axis_index("table")
    for p in range(plan_ref.shape[1]):
        tile = jnp.where(plan_ref[0, p] == me, plan_ref[1, p], tile)
    return tile


def sum_body(tables, plan_ref, own_ref, *refs):
    blocks, out_ref, total_ref = refs[: tables - 1], refs[tables - 1], refs[tables]
    bags = own_ref.shape[0]
    total_ref[...] = jnp.zeros_like(total_ref)

    def add(tile, block):
        where = pl.ds(pl.multiple_of(tile * bags, bags), bags)
        total_ref[where, :] += block.astype(jnp.float32)

    add(own_tile(plan_ref), own_ref[...])
    for block_ref in blocks:
        tile = read_mark(block_ref.at[pl.ds(bags, MARK_ROWS)])
        add(tile, block_ref[:bags, :])
    out_ref[...] = total_ref[...].astype(jnp.bfloat16)


def turn_body(cols, *refs):
    slabs, states = refs[:cols], refs[cols : 2 * cols]
    rows_ref, state_ref, wide_ref = refs[2 * cols :]
    thin = slabs[0].shape[0]
    here = lax.axis_index("col")
    for source, out_ref in ((slabs, rows_ref), (states, state_ref)):
        for k in range(cols):
            first = pl.multiple_of(origin(here, k, cols) * thin, thin)
            wide_ref[pl.ds(first, thin), :] = source[k][...].astype(jnp.float32)
        out_ref[...] = wide_ref[...].T.astype(out_ref.dtype)


def update_body(tables, chunk, plan_ref, grad_ref, counts_ref, rows_ref, state_ref, *refs):
    blocks = refs[: tables - 1]
    out_rows_ref, out_state_ref, new_rows_ref, new_state_ref, cots_ref, pair_ref, sems = refs[tables - 1 :]
    bags = blocks[0].shape[0]
    me = lax.axis_index("table")
    for p in range(plan_ref.shape[1]):
        pair_ref[step_of(plan_ref[0, p], me, tables)] = p

    def put(k, block):
        first = pl.multiple_of(pair_ref[k] * bags, bags)
        cots_ref[pl.ds(first, bags), :] = block

    tile = own_tile(plan_ref)
    put(0, grad_ref[pl.ds(pl.multiple_of(tile * bags, bags), bags), :])
    for k in range(1, tables):
        put(k, blocks[k - 1][...])

    copies = []
    for r in range(counts_ref.shape[0] // chunk):
        where = pl.ds(r * chunk, chunk)
        grad = jnp.dot(counts_ref[where, :], cots_ref[...], preferred_element_type=jnp.float32)
        state = state_ref[where, :].astype(jnp.float32) + grad * grad
        rows = rows_ref[where, :].astype(jnp.float32)
        new_state_ref[where, :] = state
        new_rows_ref[where, :] = (
            rows - LEARN_RATE * grad / (jnp.sqrt(state) + EPSILON)
        ).astype(jnp.bfloat16)
        for i, (src, dst) in enumerate(((new_state_ref, out_state_ref), (new_rows_ref, out_rows_ref))):
            copy = pltpu.make_async_copy(src.at[where], dst.at[where], sems.at[r, i])
            copy.start()
            copies.append(copy)
    for copy in copies:
        copy.wait()


def per_device(embedding, accumulator, pair_rows, pair_len, pair_dest, pair_tile, pooled_grad):
    tables, cols = lax.axis_size("table"), lax.axis_size("col")
    pairs, bags, looks = pair_rows.shape
    thin = embedding.shape[1]
    width = thin * cols
    rows = embedding.shape[0] // cols
    span = min(8, pairs)
    chunk = min(256, rows)
    shape, near = jax.ShapeDtypeStruct, pltpu.VMEM
    bf16 = jnp.bfloat16
    mega = 1 << 20
    spare = pairs * bags * width * 2
    big = 4 * mega + rows * pairs * bags * 2 + 4 * spare + 12 * rows * width

    plan = jnp.concatenate([pair_dest, pair_tile])

    def over_col(parts):
        moved = {k: lax.ppermute(parts[k], "col", pairs_of(k, cols)) for k in steps(cols)}
        return [parts[0]] + [moved[k] for k in range(1, cols)]

    slabs = call(
        functools.partial(split_body, cols, rows),
        [near((thin, rows), bf16)] * cols,
        [HBM],
        [VMEM] * cols,
        (far(embedding.T),),
        scratch=[pltpu.SemaphoreType.DMA((cols,))],
        limit=8 * mega,
    )
    slabs = over_col(slabs)
    counts, *states = call(
        functools.partial(count_body, cols),
        [near((rows, pairs * bags), bf16)] + [near((thin, rows), bf16)] * cols,
        [HBM, HBM, HBM],
        [VMEM] * (1 + cols),
        (far(accumulator.T), far(jnp.transpose(pair_rows, (0, 2, 1))), far(pair_len)),
        scratch=[
            pltpu.VMEM((pairs, looks, bags), jnp.int32),
            pltpu.VMEM((pairs, bags), jnp.int32),
            pltpu.VMEM((cols, thin, rows), jnp.float32),
            pltpu.SemaphoreType.DMA((cols + 2,)),
        ],
        limit=8 * mega + rows * pairs * bags * 2,
    )
    states = over_col(states)

    sent = call(
        functools.partial(pool_body, tables, cols, span),
        [near((bags, width), bf16)] + [near((bags + MARK_ROWS, width), bf16)] * (tables - 1),
        [SMEM, VMEM] + [VMEM] * cols,
        [VMEM] * tables,
        (plan, counts, *slabs),
        scratch=[
            pltpu.VMEM((width, rows), bf16),
            pltpu.VMEM((pairs, bags, width), bf16),
            pltpu.SMEM((pairs,), jnp.int32),
        ],
        limit=big,
        flops=2 * rows * width * pairs * bags,
    )
    own_block = sent[0]
    arrived, returned = {}, {}
    for kind, k in sequence(tables):
        if kind == "part":
            arrived[k] = lax.ppermute(sent[k], "table", pairs_of(k, tables))
        else:
            picked = call(
                functools.partial(pick_body, 1, bags),
                [near((bags, width), bf16)],
                [VMEM, VMEM],
                [VMEM],
                (arrived[k], pooled_grad),
                limit=8 * mega + 2 * spare,
            )
            returned[k] = lax.ppermute(picked[0], "table", back_of(k, tables))

    pooled = call(
        functools.partial(sum_body, tables),
        shape(pooled_grad.shape, bf16),
        [SMEM, VMEM] + [VMEM] * (tables - 1),
        VMEM,
        (plan, own_block, *[arrived[k] for k in range(1, tables)]),
        scratch=[pltpu.VMEM(pooled_grad.shape, jnp.float32)],
        limit=8 * mega + 2 * spare,
    )

    turned = call(
        functools.partial(turn_body, cols),
        [near((rows, width), bf16), near((rows, width), bf16)],
        [VMEM] * (2 * cols),
        [VMEM, VMEM],
        (*slabs, *states),
        scratch=[pltpu.VMEM((width, rows), jnp.float32)],
        limit=16 * mega,
    )
    new_rows, new_state = call(
        functools.partial(update_body, tables, chunk),
        [shape((rows, width), bf16), shape((rows, width), jnp.float32)],
        [SMEM, VMEM, VMEM, VMEM, VMEM] + [VMEM] * (tables - 1),
        [ANY, ANY],
        (plan, pooled_grad, counts, *turned, *[returned[k] for k in range(1, tables)]),
        scratch=[
            pltpu.VMEM((rows, width), bf16),
            pltpu.VMEM((rows, width), jnp.float32),
            pltpu.VMEM((pairs * bags, width), bf16),
            pltpu.SMEM((pairs,), jnp.int32),
            pltpu.SemaphoreType.DMA((rows // chunk, 2)),
        ],
        limit=big,
        flops=2 * rows * width * pairs * bags,
    )
    return (pooled, new_rows, new_state)


def solution(mesh):
    return jax.shard_map(
        per_device,
        mesh=mesh,
        in_specs=(
            P("table", "col"),
            P("table", "col"),
            P(("table", "col"), None, None),
            P(("table", "col"), None),
            P(("table", "col"), None),
            P(("table", "col"), None),
            P(("table", "col"), None),
        ),
        out_specs=(P(("table", "col"), None), P(("table", "col"), None), P(("table", "col"), None)),
        check_vma=False,
    )
```

```python
import functools

import jax
import jax.numpy as jnp
from jax import lax
from jax.experimental import pallas as pl
from jax.experimental.pallas import tpu as pltpu
from jax.sharding import PartitionSpec as P


LEARN_RATE = 0.3
EPSILON = 1e-08
MARK_ROWS = 8
LATE = 2

ANY = pl.BlockSpec(memory_space=pl.ANY)
HBM = pl.BlockSpec(memory_space=pltpu.HBM)
VMEM = pl.BlockSpec(memory_space=pltpu.VMEM)
SMEM = pl.BlockSpec(memory_space=pltpu.SMEM)


def pairs_of(k, n):
    assert n & (n - 1) == 0, n
    return [(i, i ^ k) for i in range(n)]


def call(body, out_shape, in_specs, out_specs, args, scratch=(), limit=None, flops=0):
    size = sum(a.size * a.dtype.itemsize for a in args)
    return pl.pallas_call(
        body,
        out_shape=out_shape,
        in_specs=in_specs,
        out_specs=out_specs,
        scratch_shapes=scratch,
        compiler_params=pltpu.CompilerParams(vmem_limit_bytes=limit),
        cost_estimate=pl.CostEstimate(flops=flops, bytes_accessed=size, transcendentals=0),
    )(*args)


def far(x):
    return pltpu.with_memory_space_constraint(x, pltpu.HBM)


def sequence(n):
    top = [k for k in range(1, n) if 2 * k >= n]
    low = [k for k in range(1, n) if 2 * k < n]
    mixed = top[:1]
    for i in range(len(low)):
        mixed += [top[i + 1], low[i]]
    return [("part", k) for k in mixed] + [("cot", k) for k in mixed]


def split_body(count, rows, wide_ref, *refs):
    outs, sems = refs[:count], refs[count]
    me = lax.axis_index("col")
    copies = []
    for k in range(count):
        start = pl.multiple_of((me ^ k) * rows, rows)
        copies.append(pltpu.make_async_copy(wide_ref.at[:, pl.ds(start, rows)], outs[k], sems.at[k]))
        copies[k].start()
    for copy in copies:
        copy.wait()


def count_body(cols, wide_ref, rows_hbm, lens_hbm, dest_hbm, tile_hbm, counts_ref, plan_ref, *refs):
    outs = refs[:cols]
    rows_ref, lens_ref, slab_ref, dest_ref, tile_ref, sems = refs[cols:]
    pairs, looks, bags = rows_ref.shape
    width = counts_ref.shape[0]
    me = lax.axis_index("col")
    rows_copy = pltpu.make_async_copy(rows_hbm, rows_ref, sems.at[cols])
    lens_copy = pltpu.make_async_copy(lens_hbm, lens_ref, sems.at[cols + 1])
    dest_copy = pltpu.make_async_copy(dest_hbm, dest_ref, sems.at[cols + 2])
    tile_copy = pltpu.make_async_copy(tile_hbm, tile_ref, sems.at[cols + 3])
    for copy in (rows_copy, lens_copy, dest_copy, tile_copy):
        copy.start()
    copies = []
    for k in range(cols):
        start = pl.multiple_of((me ^ k) * width, width)
        copies.append(
            pltpu.make_async_copy(wide_ref.at[:, pl.ds(start, width)], slab_ref.at[k], sems.at[k])
        )
        copies[k].start()
    rows_copy.wait()
    lens_copy.wait()

    def one(p, carry):
        line = lax.broadcasted_iota(jnp.int32, (width, bags), 0)
        lens = lens_ref[pl.ds(p, 1), :]
        total = jnp.zeros((width, bags), jnp.float32)
        for look in range(looks):
            row = rows_ref[p, pl.ds(look, 1), :]
            row = jnp.where(lens > look, row, -1)
            total = total + (line == row).astype(jnp.float32)
        counts_ref[:, pl.ds(pl.multiple_of(p * bags, bags), bags)] = total.astype(jnp.bfloat16)
        return carry

    lax.fori_loop(0, pairs, one, 0)
    dest_copy.wait()
    tile_copy.wait()
    plan_ref[0:1, :] = dest_ref[...]
    plan_ref[1:2, :] = tile_ref[...]
    for k in range(cols):
        copies[k].wait()
        outs[k][...] = slab_ref[k].astype(jnp.bfloat16)


def pool_pairs(span, slabs, counts_ref, wide_ref, put):
    here = lax.axis_index("col")
    thin = slabs[0].shape[0]
    bags = counts_ref.shape[1] // span[1]
    for k, slab_ref in enumerate(slabs):
        first = pl.multiple_of(((here ^ k) % len(slabs)) * thin, thin)
        wide_ref[pl.ds(first, thin), :] = slab_ref[...]
    wide = wide_ref[...]

    def group(g, carry):
        first = pl.multiple_of(g * span[0] * bags, span[0] * bags)
        part = jnp.dot(
            wide, counts_ref[:, pl.ds(first, span[0] * bags)], preferred_element_type=jnp.float32
        )
        for s in range(span[0]):
            put(g * span[0] + s, part[:, s * bags : (s + 1) * bags].T.astype(jnp.bfloat16))
        return carry

    lax.fori_loop(0, span[1] // span[0], group, 0)


def early_body(span, counts_ref, *refs):
    slabs, parts_ref, wide_ref = refs[:-2], refs[-2], refs[-1]

    def put(p, part):
        parts_ref[p] = part

    pool_pairs(span, slabs, counts_ref, wide_ref, put)


def pool_body(tables, cols, span, plan_ref, counts_ref, early_ref, *refs):
    slabs, refs = refs[: cols // 2], refs[cols // 2 :]
    wide_ref, parts_ref, pair_ref = refs[-3:]
    outs = refs[:-3]
    pairs, bags, half = parts_ref.shape
    me = lax.axis_index("table")
    for p in range(pairs):
        pair_ref[plan_ref[0, p] ^ me] = p

    def put(p, part):
        parts_ref[p] = part

    pool_pairs(span, slabs, counts_ref, wide_ref, put)
    side = lax.axis_index("col") // (cols // 2)
    mine = pl.ds(pl.multiple_of(side * bags, bags), bags)
    other = pl.ds(pl.multiple_of((1 - side) * bags, bags), bags)
    lane = lax.broadcasted_iota(jnp.int32, (MARK_ROWS, half), 1)
    for k in range(tables):
        p = pair_ref[k]
        out_ref = outs[k]
        out_ref[mine, :] = early_ref[p]
        out_ref[other, :] = parts_ref[p]
        if k:
            tile = plan_ref[1, p]
            mark = jnp.where(lane < half // 2, tile % 128, tile // 128)
            out_ref[pl.ds(2 * bags, MARK_ROWS), :] = mark.astype(jnp.float32).astype(jnp.bfloat16)


def read_mark(message_ref, bags):
    mark = message_ref[2 * bags :, :].astype(jnp.float32)
    low = lax.broadcasted_iota(jnp.int32, mark.shape, 1) < mark.shape[1] // 2
    units = jnp.max(jnp.where(low, mark, 0.0)).astype(jnp.int32)
    return jnp.max(jnp.where(low, 0.0, mark)).astype(jnp.int32) * 128 + units


def pick_body(bags, grad_ref, message_ref, out_ref):
    tile = read_mark(message_ref, bags)
    out_ref[...] = grad_ref[pl.ds(pl.multiple_of(tile * bags, bags), bags), :]


def own_tile(plan_ref):
    tile, me = 0, lax.axis_index("table")
    for p in range(plan_ref.shape[1]):
        tile = jnp.where(plan_ref[0, p] == me, plan_ref[1, p], tile)
    return tile


def sum_body(plan_ref, own_ref, messages, out_ref, total_ref):
    bags, half = own_ref.shape[0] // 2, own_ref.shape[1]
    tiles = [own_tile(plan_ref)] + [read_mark(message, bags) for message in messages]
    spots = [pl.ds(pl.multiple_of(tile * bags, bags), bags) for tile in tiles]
    out_ref[...] = jnp.zeros_like(out_ref)
    for spot in spots:
        total_ref[spot, :] = jnp.zeros((bags, 2 * half), jnp.float32)
    for spot, block_ref in zip(spots, (own_ref, *messages), strict=True):
        total_ref[spot, :half] += block_ref[:bags, :].astype(jnp.float32)
        total_ref[spot, half:] += block_ref[bags : 2 * bags, :].astype(jnp.float32)
    for spot in spots:
        out_ref[spot, :] = total_ref[spot, :].astype(jnp.bfloat16)


def turn_body(slabs, states, rows_ref, state_ref, wide_ref):
    cols = len(slabs)
    thin = slabs[0].shape[0]
    here = lax.axis_index("col")
    for source, out_ref in ((slabs, rows_ref), (states, state_ref)):
        for k in range(cols):
            first = pl.multiple_of((here ^ k) * thin, thin)
            wide_ref[pl.ds(first, thin), :] = source[k][...].astype(jnp.float32)
        out_ref[...] = wide_ref[...].T.astype(out_ref.dtype)


def ready_body(ahead, late, chunk, plan_ref, grad_ref, counts_ref, messages, sum_ref, counts_late_ref, cots_ref, pair_ref):
    bags = counts_late_ref.shape[1] // len(late)
    me = lax.axis_index("table")
    for p in range(plan_ref.shape[1]):
        pair_ref[plan_ref[0, p] ^ me] = p

    def spot(k):
        return pl.ds(pl.multiple_of(pair_ref[k] * bags, bags), bags)

    for i, k in enumerate(late):
        counts_late_ref[:, i * bags : (i + 1) * bags] = counts_ref[:, spot(k)]
        cots_ref[spot(k), :] = jnp.zeros((bags, cots_ref.shape[1]), cots_ref.dtype)
    tile = own_tile(plan_ref)
    cots_ref[spot(0), :] = grad_ref[pl.ds(pl.multiple_of(tile * bags, bags), bags), :]
    for k, message in zip(ahead, messages, strict=True):
        cots_ref[spot(k), :] = message[...]

    def one(r, carry):
        where = pl.ds(pl.multiple_of(r * chunk, chunk), chunk)
        sum_ref[where, :] = jnp.dot(
            counts_ref[where, :], cots_ref[...], preferred_element_type=jnp.float32
        )
        return carry

    lax.fori_loop(0, counts_ref.shape[0] // chunk, one, 0)


def finish_body(ahead, late, chunk, cols, plan_ref, own_ref, grad_ref, counts_ref, *refs):
    parts = len(ahead) + len(late)
    messages, refs = refs[:parts], refs[parts:]
    cots, refs = refs[: len(ahead)], refs[len(ahead) :]
    slabs, states, refs = refs[:cols], refs[cols : 2 * cols], refs[2 * cols :]
    pooled_out, rows_ref, state_ref, sum_ref, late_ref = refs[:5]
    pooled_ref, total_ref, wide_ref, cots_ref, pair_ref, sem = refs[5:]
    sum_body(plan_ref, own_ref, messages, pooled_ref, total_ref)
    copy = pltpu.make_async_copy(pooled_ref, pooled_out, sem)
    copy.start()
    ready_body(ahead, late, chunk, plan_ref, grad_ref, counts_ref, cots, sum_ref, late_ref, cots_ref, pair_ref)
    turn_body(slabs, states, rows_ref, state_ref, wide_ref)
    copy.wait()


def update_body(chunk, sum_ref, counts_ref, rows_ref, state_ref, *refs):
    messages = refs[:-6]
    out_rows_ref, out_state_ref, new_rows_ref, new_state_ref, cots_ref, sems = refs[-6:]
    bags = counts_ref.shape[1] // len(messages)
    for i, message in enumerate(messages):
        cots_ref[i * bags : (i + 1) * bags, :] = message[...]
    copies = []
    for r in range(counts_ref.shape[0] // chunk):
        where = pl.ds(r * chunk, chunk)
        grad = sum_ref[where, :] + jnp.dot(
            counts_ref[where, :], cots_ref[...], preferred_element_type=jnp.float32
        )
        state = state_ref[where, :].astype(jnp.float32) + grad * grad
        rows = rows_ref[where, :].astype(jnp.float32)
        new_state_ref[where, :] = state
        new_rows_ref[where, :] = (
            rows - LEARN_RATE * grad / (jnp.sqrt(state) + EPSILON)
        ).astype(jnp.bfloat16)
        for i, (src, dst) in enumerate(((new_state_ref, out_state_ref), (new_rows_ref, out_rows_ref))):
            copy = pltpu.make_async_copy(src.at[where], dst.at[where], sems.at[r, i])
            copy.start()
            copies.append(copy)
    for copy in copies:
        copy.wait()


def per_device(embedding, accumulator, pair_rows, pair_len, pair_dest, pair_tile, pooled_grad):
    tables, cols = lax.axis_size("table"), lax.axis_size("col")
    pairs, bags, looks = pair_rows.shape
    thin = embedding.shape[1]
    width = thin * cols
    rows = embedding.shape[0] // cols
    span = min(8, pairs)
    chunk = min(256, rows)
    shape, near = jax.ShapeDtypeStruct, pltpu.VMEM
    bf16 = jnp.bfloat16
    mega = 1 << 20
    spare = pairs * bags * width * 2
    big = 12 * mega + 3 * spare

    def over_col(parts):
        moved = {k: lax.ppermute(parts[k], "col", pairs_of(k, cols)) for k in range(1, cols)}
        return [parts[0]] + [moved[k] for k in range(1, cols)]

    slabs = call(
        functools.partial(split_body, cols, rows),
        [near((thin, rows), bf16)] * cols,
        [HBM],
        [VMEM] * cols,
        (far(embedding.T),),
        scratch=[pltpu.SemaphoreType.DMA((cols,))],
        limit=8 * mega,
    )
    slabs = over_col(slabs)
    counts, plan, *states = call(
        functools.partial(count_body, cols),
        [near((rows, pairs * bags), bf16), near((2, pairs), jnp.int32)] + [near((thin, rows), bf16)] * cols,
        [HBM] * 5,
        [VMEM] * (2 + cols),
        (
            far(accumulator.T),
            far(jnp.transpose(pair_rows, (0, 2, 1))),
            far(pair_len),
            far(pair_dest),
            far(pair_tile),
        ),
        scratch=[
            pltpu.VMEM((pairs, looks, bags), jnp.int32),
            pltpu.VMEM((pairs, bags), jnp.int32),
            pltpu.VMEM((cols, thin, rows), jnp.float32),
            pltpu.VMEM((1, pairs), jnp.int32),
            pltpu.VMEM((1, pairs), jnp.int32),
            pltpu.SemaphoreType.DMA((cols + 4,)),
        ],
        limit=8 * mega,
    )
    states = over_col(states)

    half, count = width // 2, (span, pairs)
    early = call(
        functools.partial(early_body, count),
        near((pairs, bags, half), bf16),
        [VMEM] * (1 + cols // 2),
        VMEM,
        (counts, *slabs[: cols // 2]),
        scratch=[pltpu.VMEM((half, rows), bf16)],
        limit=big,
        flops=rows * width * pairs * bags,
    )
    own_block, *blocks = call(
        functools.partial(pool_body, tables, cols, count),
        [near((2 * bags + (MARK_ROWS if k else 0), half), bf16) for k in range(tables)],
        [SMEM, VMEM, VMEM] + [VMEM] * (cols // 2),
        [VMEM] * tables,
        (plan, counts, early, *slabs[cols // 2 :]),
        scratch=[
            pltpu.VMEM((half, rows), bf16),
            pltpu.VMEM((pairs, bags, half), bf16),
            pltpu.SMEM((pairs,), jnp.int32),
        ],
        limit=big,
        flops=rows * width * pairs * bags,
    )
    arrived, returned = {}, {}
    for kind, k in sequence(tables):
        if kind == "part":
            arrived[k] = lax.ppermute(blocks[k - 1], "table", pairs_of(k, tables))
        else:
            picked = call(
                functools.partial(pick_body, bags),
                near((bags, width), bf16),
                [VMEM, VMEM],
                VMEM,
                (pooled_grad, arrived[k]),
                limit=8 * mega,
            )
            returned[k] = lax.ppermute(picked, "table", pairs_of(k, tables))

    cut = max(len(returned) - LATE, 0)
    ahead, late = list(returned)[:cut], list(returned)[cut:]
    pooled, *turned, so_far, counts_late = call(
        functools.partial(
            finish_body, ahead, late, min(512, rows), cols
        ),
        [shape(pooled_grad.shape, bf16)]
        + [near((rows, width), bf16)] * 2
        + [near((rows, width), jnp.float32), near((rows, len(late) * bags), bf16)],
        [SMEM] + [VMEM] * (3 + len(arrived) + len(ahead) + 2 * cols),
        [ANY] + [VMEM] * 4,
        (
            plan,
            own_block,
            pooled_grad,
            counts,
            *arrived.values(),
            *[returned[k] for k in ahead],
            *slabs,
            *states,
        ),
        scratch=[
            pltpu.VMEM(pooled_grad.shape, bf16),
            pltpu.VMEM(pooled_grad.shape, jnp.float32),
            pltpu.VMEM((width, rows), jnp.float32),
            pltpu.VMEM((pairs * bags, width), bf16),
            pltpu.SMEM((pairs,), jnp.int32),
            pltpu.SemaphoreType.DMA,
        ],
        limit=big,
        flops=2 * rows * width * pairs * bags,
    )
    new_rows, new_state = call(
        functools.partial(update_body, chunk),
        [shape((rows, width), bf16), shape((rows, width), jnp.float32)],
        [VMEM] * (4 + len(late)),
        [ANY, ANY],
        (so_far, counts_late, *turned, *[returned[k] for k in late]),
        scratch=[
            pltpu.VMEM((rows, width), bf16),
            pltpu.VMEM((rows, width), jnp.float32),
            pltpu.VMEM((len(late) * bags, width), bf16),
            pltpu.SemaphoreType.DMA((rows // chunk, 2)),
        ],
        limit=big,
        flops=2 * rows * width * len(late) * bags,
    )
    return (pooled, new_rows, new_state)


def solution(mesh):
    return jax.shard_map(
        per_device,
        mesh=mesh,
        in_specs=(
            P("table", "col"),
            P("table", "col"),
            P(("table", "col"), None, None),
            P(("table", "col"), None),
            P(("table", "col"), None),
            P(("table", "col"), None),
            P(("table", "col"), None),
        ),
        out_specs=(P(("table", "col"), None), P(("table", "col"), None), P(("table", "col"), None)),
        check_vma=False,
    )
```

```python
import functools

import jax
import jax.numpy as jnp
from jax import lax
from jax.experimental import pallas as pl
from jax.experimental.pallas import tpu as pltpu
from jax.sharding import PartitionSpec as P


LEARN_RATE = 0.3
EPSILON = 1e-08
MARK_ROWS = 8
LATE = 2

ANY = pl.BlockSpec(memory_space=pl.ANY)
HBM = pl.BlockSpec(memory_space=pltpu.HBM)
VMEM = pl.BlockSpec(memory_space=pltpu.VMEM)
SMEM = pl.BlockSpec(memory_space=pltpu.SMEM)


def pairs_of(k, n):
    assert n & (n - 1) == 0, n
    return [(i, i ^ k) for i in range(n)]


def call(body, out_shape, in_specs, out_specs, args, scratch=(), limit=None, flops=0):
    size = sum(a.size * a.dtype.itemsize for a in args)
    return pl.pallas_call(
        body,
        out_shape=out_shape,
        in_specs=in_specs,
        out_specs=out_specs,
        scratch_shapes=scratch,
        compiler_params=pltpu.CompilerParams(vmem_limit_bytes=limit),
        cost_estimate=pl.CostEstimate(flops=flops, bytes_accessed=size, transcendentals=0),
    )(*args)


def far(x):
    return pltpu.with_memory_space_constraint(x, pltpu.HBM)


def sequence(n):
    top = [k for k in range(1, n) if 2 * k >= n]
    low = [k for k in range(1, n) if 2 * k < n]
    parts, cots = top[:1], top[:1]
    for i in range(len(low)):
        parts += [top[i + 1], low[i]]
        cots += [top[i + 1], low[i]] if i else [low[i], top[i + 1]]
    return [("part", k) for k in parts] + [("cot", k) for k in cots]


def batches(n):
    order = [k for kind, k in sequence(n) if kind == "cot"]
    return [order[:1]] + [order[i : i + 2] for i in range(1, len(order), 2)]


def split_body(count, rows, wide_ref, *refs):
    outs, sems = refs[:count], refs[count]
    me = lax.axis_index("col")
    copies = []
    for k in range(count):
        start = pl.multiple_of((me ^ k) * rows, rows)
        copies.append(pltpu.make_async_copy(wide_ref.at[:, pl.ds(start, rows)], outs[k], sems.at[k]))
        copies[k].start()
    for copy in copies:
        copy.wait()


def count_body(cols, wide_ref, rows_hbm, lens_hbm, dest_hbm, tile_hbm, counts_ref, plan_ref, *refs):
    outs = refs[:cols]
    rows_ref, lens_ref, slab_ref, dest_ref, tile_ref, sems = refs[cols:]
    pairs, looks, bags = rows_ref.shape
    width = counts_ref.shape[0]
    me = lax.axis_index("col")
    rows_copy = pltpu.make_async_copy(rows_hbm, rows_ref, sems.at[cols])
    lens_copy = pltpu.make_async_copy(lens_hbm, lens_ref, sems.at[cols + 1])
    dest_copy = pltpu.make_async_copy(dest_hbm, dest_ref, sems.at[cols + 2])
    tile_copy = pltpu.make_async_copy(tile_hbm, tile_ref, sems.at[cols + 3])
    for copy in (rows_copy, lens_copy, dest_copy, tile_copy):
        copy.start()
    copies = []
    for k in range(cols):
        start = pl.multiple_of((me ^ k) * width, width)
        copies.append(
            pltpu.make_async_copy(wide_ref.at[:, pl.ds(start, width)], slab_ref.at[k], sems.at[k])
        )
        copies[k].start()
    rows_copy.wait()
    lens_copy.wait()

    def one(p, carry):
        line = lax.broadcasted_iota(jnp.int32, (width, bags), 0)
        lens = lens_ref[pl.ds(p, 1), :]
        total = jnp.zeros((width, bags), jnp.float32)
        for look in range(looks):
            row = rows_ref[p, pl.ds(look, 1), :]
            row = jnp.where(lens > look, row, -1)
            total = total + (line == row).astype(jnp.float32)
        counts_ref[:, pl.ds(pl.multiple_of(p * bags, bags), bags)] = total.astype(jnp.bfloat16)
        return carry

    lax.fori_loop(0, pairs, one, 0)
    dest_copy.wait()
    tile_copy.wait()
    plan_ref[0:1, :] = dest_ref[...]
    plan_ref[1:2, :] = tile_ref[...]
    for k in range(cols):
        copies[k].wait()
        outs[k][...] = slab_ref[k].astype(jnp.bfloat16)


def pool_pairs(span, slabs, counts_ref, wide_ref, put):
    here = lax.axis_index("col")
    thin = slabs[0].shape[0]
    bags = counts_ref.shape[1] // span[1]
    for k, slab_ref in enumerate(slabs):
        first = pl.multiple_of(((here ^ k) % len(slabs)) * thin, thin)
        wide_ref[pl.ds(first, thin), :] = slab_ref[...]
    wide = wide_ref[...]

    def group(g, carry):
        first = pl.multiple_of(g * span[0] * bags, span[0] * bags)
        part = jnp.dot(
            wide, counts_ref[:, pl.ds(first, span[0] * bags)], preferred_element_type=jnp.float32
        )
        for s in range(span[0]):
            put(g * span[0] + s, part[:, s * bags : (s + 1) * bags].T.astype(jnp.bfloat16))
        return carry

    lax.fori_loop(0, span[1] // span[0], group, 0)


def early_body(span, counts_ref, *refs):
    slabs, parts_ref, wide_ref = refs[:-2], refs[-2], refs[-1]

    def put(p, part):
        parts_ref[p] = part

    pool_pairs(span, slabs, counts_ref, wide_ref, put)


def pool_body(tables, cols, span, plan_ref, counts_ref, early_ref, *refs):
    slabs, refs = refs[: cols // 2], refs[cols // 2 :]
    wide_ref, parts_ref, pair_ref = refs[-3:]
    outs = refs[:-3]
    pairs, bags, half = parts_ref.shape
    me = lax.axis_index("table")
    for p in range(pairs):
        pair_ref[plan_ref[0, p] ^ me] = p

    def put(p, part):
        parts_ref[p] = part

    pool_pairs(span, slabs, counts_ref, wide_ref, put)
    side = lax.axis_index("col") // (cols // 2)
    mine = pl.ds(pl.multiple_of(side * bags, bags), bags)
    other = pl.ds(pl.multiple_of((1 - side) * bags, bags), bags)
    lane = lax.broadcasted_iota(jnp.int32, (MARK_ROWS, half), 1)
    for k in range(tables):
        p = pair_ref[k]
        out_ref = outs[k]
        out_ref[mine, :] = early_ref[p]
        out_ref[other, :] = parts_ref[p]
        if k:
            tile = plan_ref[1, p]
            mark = jnp.where(lane < half // 2, tile % 128, tile // 128)
            out_ref[pl.ds(2 * bags, MARK_ROWS), :] = mark.astype(jnp.float32).astype(jnp.bfloat16)


def read_mark(message_ref, bags):
    mark = message_ref[2 * bags :, :].astype(jnp.float32)
    low = lax.broadcasted_iota(jnp.int32, mark.shape, 1) < mark.shape[1] // 2
    units = jnp.max(jnp.where(low, mark, 0.0)).astype(jnp.int32)
    return jnp.max(jnp.where(low, 0.0, mark)).astype(jnp.int32) * 128 + units


def pick_body(bags, grad_ref, *refs):
    half = len(refs) // 2
    for message_ref, out_ref in zip(refs[:half], refs[half:], strict=True):
        tile = read_mark(message_ref, bags)
        out_ref[...] = grad_ref[pl.ds(pl.multiple_of(tile * bags, bags), bags), :]


def own_tile(plan_ref):
    tile, me = 0, lax.axis_index("table")
    for p in range(plan_ref.shape[1]):
        tile = jnp.where(plan_ref[0, p] == me, plan_ref[1, p], tile)
    return tile


def sum_body(plan_ref, own_ref, messages, out_ref, total_ref):
    bags, half = own_ref.shape[0] // 2, own_ref.shape[1]
    tiles = [own_tile(plan_ref)] + [read_mark(message, bags) for message in messages]
    spots = [pl.ds(pl.multiple_of(tile * bags, bags), bags) for tile in tiles]
    out_ref[...] = jnp.zeros_like(out_ref)
    for spot in spots:
        total_ref[spot, :] = jnp.zeros((bags, 2 * half), jnp.float32)
    for spot, block_ref in zip(spots, (own_ref, *messages), strict=True):
        total_ref[spot, :half] += block_ref[:bags, :].astype(jnp.float32)
        total_ref[spot, half:] += block_ref[bags : 2 * bags, :].astype(jnp.float32)
    for spot in spots:
        out_ref[spot, :] = total_ref[spot, :].astype(jnp.bfloat16)


def turn_body(slabs, states, rows_ref, state_ref, wide_ref):
    cols = len(slabs)
    thin = slabs[0].shape[0]
    here = lax.axis_index("col")
    for source, out_ref in ((slabs, rows_ref), (states, state_ref)):
        for k in range(cols):
            first = pl.multiple_of((here ^ k) * thin, thin)
            wide_ref[pl.ds(first, thin), :] = source[k][...].astype(jnp.float32)
        out_ref[...] = wide_ref[...].T.astype(out_ref.dtype)


def ready_body(ahead, late, chunk, plan_ref, grad_ref, counts_ref, messages, sum_ref, counts_late_ref, cots_ref, pair_ref):
    bags = counts_late_ref.shape[1] // len(late)
    me = lax.axis_index("table")
    for p in range(plan_ref.shape[1]):
        pair_ref[plan_ref[0, p] ^ me] = p

    def spot(k):
        return pl.ds(pl.multiple_of(pair_ref[k] * bags, bags), bags)

    for i, k in enumerate(late):
        counts_late_ref[:, i * bags : (i + 1) * bags] = counts_ref[:, spot(k)]
        cots_ref[spot(k), :] = jnp.zeros((bags, cots_ref.shape[1]), cots_ref.dtype)
    tile = own_tile(plan_ref)
    cots_ref[spot(0), :] = grad_ref[pl.ds(pl.multiple_of(tile * bags, bags), bags), :]
    for k, message in zip(ahead, messages, strict=True):
        cots_ref[spot(k), :] = message[...]

    def one(r, carry):
        where = pl.ds(pl.multiple_of(r * chunk, chunk), chunk)
        sum_ref[where, :] = jnp.dot(
            counts_ref[where, :], cots_ref[...], preferred_element_type=jnp.float32
        )
        return carry

    lax.fori_loop(0, counts_ref.shape[0] // chunk, one, 0)


def finish_body(ahead, late, chunk, cols, plan_ref, own_ref, grad_ref, counts_ref, *refs):
    parts = len(ahead) + len(late)
    messages, refs = refs[:parts], refs[parts:]
    cots, refs = refs[: len(ahead)], refs[len(ahead) :]
    slabs, states, refs = refs[:cols], refs[cols : 2 * cols], refs[2 * cols :]
    pooled_out, rows_ref, state_ref, sum_ref, late_ref = refs[:5]
    pooled_ref, total_ref, wide_ref, cots_ref, pair_ref, sem = refs[5:]
    sum_body(plan_ref, own_ref, messages, pooled_ref, total_ref)
    copy = pltpu.make_async_copy(pooled_ref, pooled_out, sem)
    copy.start()
    ready_body(ahead, late, chunk, plan_ref, grad_ref, counts_ref, cots, sum_ref, late_ref, cots_ref, pair_ref)
    turn_body(slabs, states, rows_ref, state_ref, wide_ref)
    copy.wait()


def update_body(chunk, sum_ref, counts_ref, rows_ref, state_ref, *refs):
    messages = refs[:-6]
    out_rows_ref, out_state_ref, new_rows_ref, new_state_ref, cots_ref, sems = refs[-6:]
    bags = counts_ref.shape[1] // len(messages)
    for i, message in enumerate(messages):
        cots_ref[i * bags : (i + 1) * bags, :] = message[...]
    copies = []
    for r in range(counts_ref.shape[0] // chunk):
        where = pl.ds(r * chunk, chunk)
        grad = sum_ref[where, :] + jnp.dot(
            counts_ref[where, :], cots_ref[...], preferred_element_type=jnp.float32
        )
        state = state_ref[where, :].astype(jnp.float32) + grad * grad
        rows = rows_ref[where, :].astype(jnp.float32)
        new_state_ref[where, :] = state
        new_rows_ref[where, :] = (
            rows - LEARN_RATE * grad / (jnp.sqrt(state) + EPSILON)
        ).astype(jnp.bfloat16)
        for i, (src, dst) in enumerate(((new_state_ref, out_state_ref), (new_rows_ref, out_rows_ref))):
            copy = pltpu.make_async_copy(src.at[where], dst.at[where], sems.at[r, i])
            copy.start()
            copies.append(copy)
    for copy in copies:
        copy.wait()


def per_device(embedding, accumulator, pair_rows, pair_len, pair_dest, pair_tile, pooled_grad):
    tables, cols = lax.axis_size("table"), lax.axis_size("col")
    pairs, bags, looks = pair_rows.shape
    thin = embedding.shape[1]
    width = thin * cols
    rows = embedding.shape[0] // cols
    span = min(8, pairs)
    chunk = min(256, rows)
    shape, near = jax.ShapeDtypeStruct, pltpu.VMEM
    bf16 = jnp.bfloat16
    mega = 1 << 20
    spare = pairs * bags * width * 2
    big = 12 * mega + 3 * spare

    def over_col(parts):
        moved = {k: lax.ppermute(parts[k], "col", pairs_of(k, cols)) for k in range(1, cols)}
        return [parts[0]] + [moved[k] for k in range(1, cols)]

    slabs = call(
        functools.partial(split_body, cols, rows),
        [near((thin, rows), bf16)] * cols,
        [HBM],
        [VMEM] * cols,
        (far(embedding.T),),
        scratch=[pltpu.SemaphoreType.DMA((cols,))],
        limit=8 * mega,
    )
    slabs = over_col(slabs)
    counts, plan, *states = call(
        functools.partial(count_body, cols),
        [near((rows, pairs * bags), bf16), near((2, pairs), jnp.int32)] + [near((thin, rows), bf16)] * cols,
        [HBM] * 5,
        [VMEM] * (2 + cols),
        (
            far(accumulator.T),
            far(jnp.transpose(pair_rows, (0, 2, 1))),
            far(pair_len),
            far(pair_dest),
            far(pair_tile),
        ),
        scratch=[
            pltpu.VMEM((pairs, looks, bags), jnp.int32),
            pltpu.VMEM((pairs, bags), jnp.int32),
            pltpu.VMEM((cols, thin, rows), jnp.float32),
            pltpu.VMEM((1, pairs), jnp.int32),
            pltpu.VMEM((1, pairs), jnp.int32),
            pltpu.SemaphoreType.DMA((cols + 4,)),
        ],
        limit=8 * mega,
    )
    states = over_col(states)

    half, count = width // 2, (span, pairs)
    early = call(
        functools.partial(early_body, count),
        near((pairs, bags, half), bf16),
        [VMEM] * (1 + cols // 2),
        VMEM,
        (counts, *slabs[: cols // 2]),
        scratch=[pltpu.VMEM((half, rows), bf16)],
        limit=big,
        flops=rows * width * pairs * bags,
    )
    own_block, *blocks = call(
        functools.partial(pool_body, tables, cols, count),
        [near((2 * bags + (MARK_ROWS if k else 0), half), bf16) for k in range(tables)],
        [SMEM, VMEM, VMEM] + [VMEM] * (cols // 2),
        [VMEM] * tables,
        (plan, counts, early, *slabs[cols // 2 :]),
        scratch=[
            pltpu.VMEM((half, rows), bf16),
            pltpu.VMEM((pairs, bags, half), bf16),
            pltpu.SMEM((pairs,), jnp.int32),
        ],
        limit=big,
        flops=rows * width * pairs * bags,
    )
    arrived, returned = {}, {}
    for kind, k in sequence(tables):
        if kind == "part":
            arrived[k] = lax.ppermute(blocks[k - 1], "table", pairs_of(k, tables))
    for ks in batches(tables):
        picked = call(
            functools.partial(pick_body, bags),
            [near((bags, width), bf16)] * len(ks),
            [VMEM] * (1 + len(ks)),
            [VMEM] * len(ks),
            (pooled_grad, *[arrived[k] for k in ks]),
            limit=8 * mega,
        )
        for k, block in zip(ks, picked, strict=True):
            returned[k] = lax.ppermute(block, "table", pairs_of(k, tables))

    cut = max(len(returned) - LATE, 0)
    ahead, late = list(returned)[:cut], list(returned)[cut:]
    pooled, *turned, so_far, counts_late = call(
        functools.partial(
            finish_body, ahead, late, rows, cols
        ),
        [shape(pooled_grad.shape, bf16)]
        + [near((rows, width), bf16)] * 2
        + [near((rows, width), jnp.float32), near((rows, len(late) * bags), bf16)],
        [SMEM] + [VMEM] * (3 + len(arrived) + len(ahead) + 2 * cols),
        [ANY] + [VMEM] * 4,
        (
            plan,
            own_block,
            pooled_grad,
            counts,
            *arrived.values(),
            *[returned[k] for k in ahead],
            *slabs,
            *states,
        ),
        scratch=[
            pltpu.VMEM(pooled_grad.shape, bf16),
            pltpu.VMEM(pooled_grad.shape, jnp.float32),
            pltpu.VMEM((width, rows), jnp.float32),
            pltpu.VMEM((pairs * bags, width), bf16),
            pltpu.SMEM((pairs,), jnp.int32),
            pltpu.SemaphoreType.DMA,
        ],
        limit=big,
        flops=2 * rows * width * pairs * bags,
    )
    new_rows, new_state = call(
        functools.partial(update_body, chunk),
        [shape((rows, width), bf16), shape((rows, width), jnp.float32)],
        [VMEM] * (4 + len(late)),
        [ANY, ANY],
        (so_far, counts_late, *turned, *[returned[k] for k in late]),
        scratch=[
            pltpu.VMEM((rows, width), bf16),
            pltpu.VMEM((rows, width), jnp.float32),
            pltpu.VMEM((len(late) * bags, width), bf16),
            pltpu.SemaphoreType.DMA((rows // chunk, 2)),
        ],
        limit=big,
        flops=2 * rows * width * len(late) * bags,
    )
    return (pooled, new_rows, new_state)


def solution(mesh):
    return jax.shard_map(
        per_device,
        mesh=mesh,
        in_specs=(
            P("table", "col"),
            P("table", "col"),
            P(("table", "col"), None, None),
            P(("table", "col"), None),
            P(("table", "col"), None),
            P(("table", "col"), None),
            P(("table", "col"), None),
        ),
        out_specs=(P(("table", "col"), None), P(("table", "col"), None), P(("table", "col"), None)),
        check_vma=False,
    )
```
